32 devices in a mesh: replica: 4 (over y, x), seq: 8 (over z, core).
Axes of the slice: x: 2, y: 2, z: 4, core: 2. Of those that a mesh axis runs over, the one named last changes fastest.
Arguments:
- tokens: bfloat16 [4, 1024, 1536], P('replica', 'seq'), may hold values from -6 to 6
- span_order: int32 [4, 8], P('replica'), may hold values from 0 to 7, each once within a row
- w_query: bfloat16 [1536, 1536], P('seq'), may hold values from -1 to 1
- w_key: bfloat16 [1536, 768], P('seq'), may hold values from -1 to 1
- w_value: bfloat16 [1536, 768], P('seq'), may hold values from -0.15625 to 0.15625
- w_out: bfloat16 [1536, 1536], P('seq'), may hold values from -2.5 to 2.5
- attn_gain: float32 [1536], P('seq'), may hold values from 0.5 to 1.5
- w_gate: bfloat16 [1536, 4096], P('seq'), may hold values from -0.15625 to 0.15625
- w_up: bfloat16 [1536, 4096], P('seq'), may hold values from -0.15625 to 0.15625
- w_down: bfloat16 [4096, 1536], P('seq'), may hold values from -0.09375 to 0.09375
- mlp_gain: float32 [1536], P('seq'), may hold values from 0.5 to 1.5
- cotangent: bfloat16 [4, 1024, 1536], P('replica', 'seq'), may hold values from -6 to 6
Outputs:
- output: bfloat16 [4, 1024, 1536], P('replica', 'seq')
- grad_tokens: bfloat16 [4, 1024, 1536], P('replica', 'seq')
- grad_w_query: float32 [1536, 1536], P('seq')
- grad_w_key: float32 [1536, 768], P('seq')
- grad_w_value: float32 [1536, 768], P('seq')
- grad_w_out: float32 [1536, 1536], P('seq')
- grad_attn_gain: float32 [1536], P('seq')
- grad_w_gate: float32 [1536, 4096], P('seq')
- grad_w_up: float32 [1536, 4096], P('seq')
- grad_w_down: float32 [4096, 1536], P('seq')
- grad_mlp_gain: float32 [1536], P('seq')
The draws below stay inside these ranges and needn't reach their ends.
Inputs may be any that keep to these rules, and one draw needn't show every extreme that they name: Each row of span_order names every block of its sequence once.
All inputs are finite; a program needn't handle non-finite values.
Results may differ from the reference program's by a relative error of at most 0.04.
Values may be sent and summed in bfloat16 or wider, within the bound.
No kernel may reach another device: no remote copies, remote signals or barrier semaphores. Data moves between devices by JAX's collectives and lax.ppermute only.
A program may use at most 320 MiB of HBM per device.

```python
import math
import jax
import jax.numpy as jnp
from jax import lax

D = 1536
H = 16
KV = 8
HD = 96
FF = 4096
TOK_DEV = 128
SEQS = 4
LENGTH = 1024
HQ = 1536
KVW = 768
N_SEQ = 8


def draw_w_query(key, part):
    values = jax.random.normal(key, (D, H * HD), jnp.float32) / math.sqrt(D)
    return jnp.clip(values, -1.0, 1.0).astype(jnp.bfloat16)


def draw_w_key(key, part):
    values = jax.random.normal(key, (D, KV * HD), jnp.float32) / math.sqrt(D)
    return jnp.clip(values, -1.0, 1.0).astype(jnp.bfloat16)


def spiked(result, rng, source, target, parts, factor):
    def block_of(position):
        return (jnp.arange(result.shape[position]) // (result.shape[position] // parts)).reshape((-1,) + (1,) * (result.ndim - 1 - position))

    first = jax.random.permutation(rng, parts)[block_of(target)]
    far = (block_of(target) + parts // 2) % parts
    return jnp.where((block_of(source) == first) | (block_of(source) == far), factor * result, result)


def shard_levels(rng, extent, shards, low, top_value):
    loudness = 1.0
    for position, shards_of in shards:
        steps = jax.random.uniform(jax.random.fold_in(jax.random.fold_in(rng, 6), position), (shards_of,), jnp.float32, low / len(shards), top_value / len(shards))
        loudness = loudness * jnp.repeat(jnp.exp(steps), extent[position] // shards_of).reshape((-1,) + (1,) * (len(extent) - 1 - position))
    return loudness


def normal_values(key, dims, deviation, most, shards=(), kind=jnp.bfloat16):
    result = deviation * jax.random.normal(key, dims, jnp.float32)
    if shards:
        result = result * shard_levels(key, dims, shards, -0.22, 0.18)
    return jnp.clip(result, -most, most).astype(kind)


def gaussian_with(stream_key, dims, deviation, most, pieces, heavy, held_as=jnp.bfloat16):
    drawn = deviation * jax.random.normal(stream_key, dims, jnp.float32)
    if pieces:
        drawn = drawn * shard_levels(stream_key, dims, pieces, -0.22, 0.18)
    return jnp.clip(spiked(drawn, jax.random.fold_in(stream_key, 3), *heavy), -most, most).astype(held_as)


def setup_inputs(seed: int = 0) -> dict:
    splits = jax.random.split(jax.random.key(seed), 13)
    tokens = gaussian_with(splits[0], (SEQS, LENGTH, D), 1.0, 6.0, ((0, 4), (1, 8)), (1, 2, 8, 2.0))
    span_order = jax.vmap(lambda own: jax.random.permutation(own, N_SEQ))(jax.random.split(splits[1], SEQS)).reshape((SEQS, N_SEQ)).astype(jnp.int32)
    w_query = draw_w_query(jax.random.fold_in(splits[12], 71), 0)
    w_key = draw_w_key(jax.random.fold_in(splits[12], 71), 0)
    w_value = normal_values(splits[4], (D, KVW), D ** -0.5, 0.15625, ((0, 8),))
    w_out = normal_values(splits[5], (HQ, D), (max(1, 4 * H * HD // (TOK_DEV * N_SEQ))) ** -0.5, 2.5, ((0, 8),))
    attn_gain = jnp.clip(1.0 + 0.1 * jax.random.normal(splits[6], (D,), jnp.float32), 0.5, 1.5)
    w_gate = normal_values(splits[7], (D, FF), D ** -0.5, 0.15625, ((0, 8),))
    w_up = normal_values(splits[8], (D, FF), D ** -0.5, 0.15625, ((0, 8),))
    w_down = normal_values(splits[9], (FF, D), FF ** -0.5, 0.09375, ((0, 8),))
    mlp_gain = jnp.clip(1.0 + 0.1 * jax.random.normal(splits[10], (D,), jnp.float32), 0.5, 1.5)
    cotangent = normal_values(splits[11], (SEQS, LENGTH, D), 1.0, 6.0, ((0, 4), (1, 8)))
    return dict(tokens=tokens, span_order=span_order, w_query=w_query, w_key=w_key, w_value=w_value, w_out=w_out, attn_gain=attn_gain, w_gate=w_gate, w_up=w_up, w_down=w_down, mlp_gain=mlp_gain, cotangent=cotangent)


epsilon = 1e-05
rope_base = 100000.0
masked_value = -1e+30

def widen(values):
    return lax.optimization_barrier(values).astype(jnp.float32)

def rope_tables(positions):
    half_dim = HD // 2
    inverse = rope_base ** (-(jnp.arange(half_dim, dtype=jnp.float32) * 2.0) / HD)
    angles = positions.astype(jnp.float32)[:, None] * inverse[None, :]
    return (jnp.cos(angles), jnp.sin(angles))

def rotate(values, cosine, sine_table):
    half_dim = values.shape[-1] // 2
    first_half = values[..., :half_dim]
    second_half = values[..., half_dim:]
    cos_rows = cosine[:, None, :]
    sin_rows = sine_table[:, None, :]
    return jnp.concatenate([first_half * cos_rows - second_half * sin_rows, second_half * cos_rows + first_half * sin_rows], -1)

def unrotate(values, cosine, sine_table):
    half_dim = values.shape[-1] // 2
    first_half = values[..., :half_dim]
    second_half = values[..., half_dim:]
    cos_rows = cosine[:, None, :]
    sin_rows = sine_table[:, None, :]
    return jnp.concatenate([first_half * cos_rows + second_half * sin_rows, second_half * cos_rows - first_half * sin_rows], -1)

def inverse_rms(values):
    return lax.rsqrt(lax.optimization_barrier(jnp.mean(values * values, -1, keepdims=True)) + epsilon)

def norm_backward(grad_normed, normed_pre, inv_rms, gain, residual_grad):
    scaled = grad_normed * gain
    return residual_grad + inv_rms * (scaled - normed_pre * lax.optimization_barrier(jnp.mean(scaled * normed_pre, -1, keepdims=True)))

def one_sequence(weights, inputs):
    w_query, w_key, w_value, w_out, attn_gain, w_gate, w_up, w_down, mlp_gain = weights
    tokens, cotangent, span_row = inputs
    length = tokens.shape[0]
    group_size = H // KV
    factor = 1.0 / math.sqrt(HD)
    positions = (span_row[:, None] * TOK_DEV + jnp.arange(TOK_DEV, dtype=jnp.int32)[None, :]).reshape(length)
    cosine, sine_table = rope_tables(positions)
    inputs_f = tokens.astype(jnp.float32)
    inv_first = inverse_rms(inputs_f)
    pre_first = inputs_f * inv_first
    normed_first = (pre_first * attn_gain).astype(jnp.bfloat16)
    query_lin = jnp.dot(normed_first, w_query, preferred_element_type=jnp.float32).reshape(length, H, HD)
    queries = rotate(query_lin, cosine, sine_table).astype(jnp.bfloat16)
    key_lin = jnp.dot(normed_first, w_key, preferred_element_type=jnp.float32).reshape(length, KV, HD)
    key_rows = rotate(key_lin, cosine, sine_table).astype(jnp.bfloat16)
    value_rows = jnp.dot(normed_first, w_value, preferred_element_type=jnp.float32).astype(jnp.bfloat16).reshape(length, KV, HD)
    keys_f = key_rows.astype(jnp.float32)
    values_f = value_rows.astype(jnp.float32)
    query_rows = min(512, length)
    block_count = length // query_rows
    query_blocks = queries.reshape(block_count, query_rows, KV, group_size, HD)
    position_blocks = positions.reshape(block_count, query_rows)

    def masked_scores(query_part, query_pos):
        scores = jnp.einsum('tkgd,skd->kgts', query_part.astype(jnp.float32), keys_f) * factor
        visible = positions[None, None, None, :] <= query_pos[None, None, :, None]
        return (jnp.where(visible, scores, masked_value), visible)

    def forward_block(blocks):
        query_part, query_pos = blocks
        scores, visible = masked_scores(query_part, query_pos)
        highest = lax.optimization_barrier(jnp.max(scores, -1, keepdims=True))
        totals = lax.optimization_barrier(jnp.sum(jnp.where(visible, jnp.exp(scores - highest), 0.0), -1, keepdims=True))
        log_total = highest + jnp.log(totals)
        probabilities = jnp.where(visible, jnp.exp(scores - log_total), 0.0).astype(jnp.bfloat16)
        mixed_out = jnp.einsum('kgts,skd->tkgd', widen(probabilities), values_f)
        return (mixed_out.astype(jnp.bfloat16), log_total[..., 0])
    attn_blocks, log_totals = lax.map(forward_block, (query_blocks, position_blocks))
    attention = attn_blocks.reshape(length, H * HD)
    middle = inputs_f + jnp.dot(attention, w_out, preferred_element_type=jnp.float32)
    inv_second = inverse_rms(middle)
    pre_second = middle * inv_second
    normed_second = (pre_second * mlp_gain).astype(jnp.bfloat16)
    gate_act = jnp.dot(normed_second, w_gate, preferred_element_type=jnp.float32)
    up_proj = jnp.dot(normed_second, w_up, preferred_element_type=jnp.float32)
    sigmoid = jax.nn.sigmoid(gate_act)
    hidden = (gate_act * sigmoid * up_proj).astype(jnp.bfloat16)
    output = (middle + jnp.dot(hidden, w_down, preferred_element_type=jnp.float32)).astype(jnp.bfloat16)
    grad_w_down = jnp.dot(hidden.T, cotangent, preferred_element_type=jnp.float32)
    grad_hidden = jnp.dot(cotangent, w_down.T, preferred_element_type=jnp.float32)
    grad_gate = (grad_hidden * up_proj * sigmoid * (1.0 + gate_act * (1.0 - sigmoid))).astype(jnp.bfloat16)
    grad_up = (grad_hidden * gate_act * sigmoid).astype(jnp.bfloat16)
    grad_w_gate = jnp.dot(normed_second.T, grad_gate, preferred_element_type=jnp.float32)
    grad_w_up = jnp.dot(normed_second.T, grad_up, preferred_element_type=jnp.float32)
    grad_normed_second = jnp.dot(grad_gate, w_gate.T, preferred_element_type=jnp.float32) + jnp.dot(grad_up, w_up.T, preferred_element_type=jnp.float32)
    grad_mlp_gain = lax.optimization_barrier(jnp.sum(grad_normed_second * pre_second, 0))
    grad_middle = norm_backward(grad_normed_second, pre_second, inv_second, mlp_gain, cotangent.astype(jnp.float32))
    grad_mid_round = grad_middle.astype(jnp.bfloat16)
    grad_w_out = jnp.dot(attention.T, grad_mid_round, preferred_element_type=jnp.float32)
    grad_attention = jnp.dot(grad_mid_round, w_out.T, preferred_element_type=jnp.float32)
    delta_rows = lax.optimization_barrier(jnp.sum(grad_attention.reshape(length, KV, group_size, HD) * attention.astype(jnp.float32).reshape(length, KV, group_size, HD), -1))
    grad_attn_round = grad_attention.astype(jnp.bfloat16).reshape(block_count, query_rows, KV, group_size, HD)
    delta_blocks = jnp.transpose(delta_rows.reshape(block_count, query_rows, KV, group_size), (0, 2, 3, 1))

    def backward_block(carried, blocks):
        key_sum, value_sum = carried
        query_part, query_pos, log_part, grad_part, delta_part = blocks
        scores, visible = masked_scores(query_part, query_pos)
        probs_full = jnp.where(visible, jnp.exp(scores - log_part[..., None]), 0.0)
        grad_wide = grad_part.astype(jnp.float32)
        grad_probs = jnp.einsum('tkgd,skd->kgts', grad_wide, values_f)
        grad_scores = widen((factor * probs_full * (grad_probs - delta_part[..., None])).astype(jnp.bfloat16))
        probs_round = widen(probs_full.astype(jnp.bfloat16))
        grad_query_part = jnp.einsum('kgts,skd->tkgd', grad_scores, keys_f)
        key_sum = key_sum + jnp.einsum('kgts,tkgd->skd', grad_scores, query_part.astype(jnp.float32))
        value_sum = value_sum + jnp.einsum('kgts,tkgd->skd', probs_round, grad_wide)
        return ((key_sum, value_sum), grad_query_part)
    zero_keys = jnp.zeros((length, KV, HD), jnp.float32)
    (key_sum, value_sum), grad_query_blocks = lax.scan(backward_block, (zero_keys, zero_keys), (query_blocks, position_blocks, log_totals, grad_attn_round, delta_blocks))
    grad_queries = unrotate(grad_query_blocks.reshape(length, H, HD), cosine, sine_table).reshape(length, H * HD).astype(jnp.bfloat16)
    grad_keys = unrotate(key_sum, cosine, sine_table).reshape(length, KV * HD).astype(jnp.bfloat16)
    grad_values = value_sum.reshape(length, KV * HD).astype(jnp.bfloat16)
    grad_w_query = jnp.dot(normed_first.T, grad_queries, preferred_element_type=jnp.float32)
    grad_w_key = jnp.dot(normed_first.T, grad_keys, preferred_element_type=jnp.float32)
    grad_w_value = jnp.dot(normed_first.T, grad_values, preferred_element_type=jnp.float32)
    grad_normed_first = jnp.dot(grad_queries, w_query.T, preferred_element_type=jnp.float32) + jnp.dot(grad_keys, w_key.T, preferred_element_type=jnp.float32) + jnp.dot(grad_values, w_value.T, preferred_element_type=jnp.float32)
    grad_attn_gain = lax.optimization_barrier(jnp.sum(grad_normed_first * pre_first, 0))
    grad_tokens = norm_backward(grad_normed_first, pre_first, inv_first, attn_gain, grad_middle).astype(jnp.bfloat16)
    return (output, grad_tokens, (grad_w_query, grad_w_key, grad_w_value, grad_w_out, grad_attn_gain, grad_w_gate, grad_w_up, grad_w_down, grad_mlp_gain))

def reference(tokens, span_order, w_query, w_key, w_value, w_out, attn_gain, w_gate, w_up, w_down, mlp_gain, cotangent):
    weights = (w_query, w_key, w_value, w_out, attn_gain, w_gate, w_up, w_down, mlp_gain)

    def scan_step(totals, inputs):
        output, grad_tokens, gradients = one_sequence(weights, inputs)
        return (tuple((total_item + grad_item for total_item, grad_item in zip(totals, gradients))), (output, grad_tokens))
    zero_grads = tuple((jnp.zeros(weight_item.shape, jnp.float32) for weight_item in weights))
    totals, (outputs, grad_inputs) = lax.scan(scan_step, zero_grads, (tokens, cotangent, span_order))
    return (outputs, grad_inputs, totals[0], totals[1], totals[2], totals[3], totals[4], totals[5], totals[6], totals[7], totals[8])
```

```python
import math

import jax
import jax.numpy as jnp
from jax import lax
from jax.sharding import PartitionSpec as P

H = 16
KV = 8
HD = 96


epsilon = 1e-05
rope_base = 100000.0
masked_value = -1e30
f32 = jnp.float32
bf16 = jnp.bfloat16


def rope_tables(positions):
    half_dim = HD // 2
    inverse = rope_base ** (-(jnp.arange(half_dim, dtype=f32) * 2.0) / HD)
    angles = positions.astype(f32)[:, None] * inverse[None, :]
    return (jnp.cos(angles), jnp.sin(angles))


def rotate(values, cosine, sine_table):
    half_dim = values.shape[-1] // 2
    first_half = values[..., :half_dim]
    second_half = values[..., half_dim:]
    cos_rows = cosine[:, None, :]
    sin_rows = sine_table[:, None, :]
    return jnp.concatenate(
        [
            first_half * cos_rows - second_half * sin_rows,
            second_half * cos_rows + first_half * sin_rows,
        ],
        -1,
    )


def unrotate(values, cosine, sine_table):
    return rotate(values, cosine, -sine_table)


def inverse_rms(values):
    return lax.rsqrt(jnp.mean(values * values, -1, keepdims=True) + epsilon)


def norm_backward(grad_normed, normed_pre, inv_rms, gain, residual_grad):
    scaled = grad_normed * gain
    return residual_grad + inv_rms * (
        scaled - normed_pre * jnp.mean(scaled * normed_pre, -1, keepdims=True)
    )


def dot(a, b):
    return jnp.dot(a, b, preferred_element_type=f32)


def dot_t(a, b):
    return lax.dot_general(a, b, (((1,), (1,)), ((), ())), preferred_element_type=f32)


def dot_first(a, b):
    return lax.dot_general(a, b, (((0,), (0,)), ((), ())), preferred_element_type=f32)


class Ring:
    def __init__(self):
        self.planes = lax.axis_size("replica")
        self.seqs = lax.axis_size("seq")
        self.lows = self.seqs // self.planes
        self.k = lax.axis_index("replica")
        self.j = lax.axis_index("seq")
        self.hi = self.j // self.lows
        self.lo = self.j % self.lows

    def move(self, value, target):
        pairs = []
        for r in range(self.planes):
            for h in range(self.planes):
                for l in range(self.lows):
                    r2, h2, l2 = target(r, h, l)
                    pairs.append(
                        (
                            r * self.seqs + h * self.lows + l,
                            r2 * self.seqs + h2 * self.lows + l2,
                        )
                    )
        return lax.ppermute(value, ("replica", "seq"), pairs)

    def peer(self, value, i):
        if i == 0:
            return value
        return self.move(value, lambda r, h, l: (r ^ i, h, l))

    def gather(self, value):
        return [self.peer(value, i) for i in range(self.planes)]

    def exchange(self, values):
        return [self.peer(value, i) for i, value in enumerate(values)]

    def spread(self, value):
        n = self.planes
        rows = value.shape[0] // n
        held = self.exchange([value[i * rows : (i + 1) * rows] for i in range(n)])
        held = xor_order(held, self.k ^ self.hi)
        got = [
            held[i] if i == 0 else self.move(held[i], lambda r, h, l: (r, h ^ i, l))
            for i in range(n)
        ]
        return jnp.concatenate(got, 0)

    def collect(self, value):
        n = self.planes
        rows = value.shape[0] // n
        parts = [value[i * rows : (i + 1) * rows] for i in range(n)]
        parts = xor_order(parts, self.k ^ self.hi)
        got = [self.move(parts[i], lambda r, h, l: (h, r ^ i, l)) for i in range(n)]
        got = xor_order(got, self.k ^ self.hi)
        return jnp.concatenate(got, 0)


def xor_order(values, u):
    values = list(values)
    bit = 1
    while bit < len(values):
        flip = (u & bit) != 0
        values = [
            jnp.where(flip, values[i ^ bit], values[i]) for i in range(len(values))
        ]
        bit *= 2
    return values


def on_device(
    tokens,
    span_order,
    w_query,
    w_key,
    w_value,
    w_out,
    attn_gain,
    w_gate,
    w_up,
    w_down,
    mlp_gain,
    cotangent,
):
    ring = Ring()
    n, seqs, lows, k = ring.planes, ring.seqs, ring.lows, ring.k
    block = tokens.shape[1]
    width = tokens.shape[2]
    rows = block * n
    piece = block // n
    heads = H // n
    kvs = KV // n
    group_size = H // KV
    factor = 1.0 / math.sqrt(HD)
    shard = w_query.shape[0]
    units = w_down.shape[0]
    sub = units // n

    def columns(weight, count):
        return lax.dynamic_slice_in_dim(weight, k * count, count, 1)

    def gather_seq(value):
        return lax.all_gather(value, "seq", axis=0, tiled=True)

    def scatter_seq(value):
        return lax.psum_scatter(value, "seq", scatter_dimension=0, tiled=True)

    hq, hk = heads * HD, kvs * HD
    gains_hi = [g.astype(bf16) for g in (attn_gain, mlp_gain)]
    gains_lo = [(g - h.astype(f32)).astype(bf16) for g, h in zip((attn_gain, mlp_gain), gains_hi)]
    gain_cols = jnp.pad(jnp.stack(gains_hi + gains_lo, 1), ((0, 0), (0, 124)))
    slab = jnp.concatenate(
        [columns(w_query, hq), columns(w_key, hk), columns(w_value, hk), gain_cols], 1
    )
    full_qkv = gather_seq(slab)
    width_out = width // n
    out_quarter = gather_seq(columns(w_out, width_out))

    def unit_columns(weight):
        parts = weight.reshape(shard, seqs, n, sub)
        return lax.dynamic_index_in_dim(parts, k, 2, False).reshape(shard, seqs * sub)

    gate_up = gather_seq(jnp.concatenate([unit_columns(w_gate), unit_columns(w_up)], 1))
    down = gather_seq(lax.dynamic_slice_in_dim(w_down, k * sub, sub, 0))

    span_row = ring.move(span_order, lambda r, h, l: (h, r, l))[0]
    mine = ring.spread(tokens[0])
    all_tokens = jnp.concatenate(ring.gather(mine), 0)
    mine_cot = ring.spread(cotangent[0])
    all_cot = jnp.concatenate(ring.gather(mine_cot), 0)

    def positions_of(lo):
        i = jnp.arange(n, dtype=jnp.int32)[:, None, None]
        j = jnp.arange(n, dtype=jnp.int32)[None, :, None]
        t = jnp.arange(piece, dtype=jnp.int32)[None, None, :]
        spans = span_row[(ring.hi ^ j) * lows + lo]
        return (spans * block + (ring.hi ^ k ^ i) * piece + t).reshape(rows)

    query_positions = positions_of(ring.lo)
    key_positions = jnp.concatenate([positions_of(ring.lo ^ e) for e in range(lows)])
    cosine, sine_table = rope_tables(query_positions)

    gain_part = full_qkv[:, hq + 2 * hk :].astype(f32)
    gain_first = gain_part[:, 0] + gain_part[:, 2]
    gain_second = gain_part[:, 1] + gain_part[:, 3]

    inputs_f = all_tokens.astype(f32)
    inv_all = inverse_rms(inputs_f)
    pre_all = inputs_f * inv_all
    normed_first = (pre_all * gain_first).astype(bf16)
    lin = dot(normed_first, full_qkv[:, : hq + 2 * hk])
    queries = rotate(lin[:, :hq].reshape(rows, heads, HD), cosine, sine_table).astype(bf16)
    key_local = (
        rotate(lin[:, hq : hq + hk].reshape(rows, kvs, HD), cosine, sine_table)
        .astype(bf16)
        .reshape(rows, hk)
    )
    value_local = lin[:, hq + hk :].astype(bf16)
    both = jnp.concatenate([key_local, value_local], 1)

    def low_peer(value, e):
        if e == 0:
            return value
        return ring.move(value, lambda r, h, l: (r, h, l ^ e))

    both_all = jnp.concatenate([low_peer(both, e) for e in range(lows)], 0)
    length = rows * lows
    keys = both_all[:, :hk].reshape(length, kvs, HD)
    values = both_all[:, hk:].reshape(length, kvs, HD)
    query_heads = queries.reshape(rows, kvs, group_size, HD)
    visible = (key_positions[None, :] <= query_positions[:, None])[None, None]

    scores = jnp.einsum("tkgd,skd->kgts", query_heads, keys, preferred_element_type=f32) * factor
    scores = jnp.where(visible, scores, masked_value)
    highest = jnp.max(scores, -1, keepdims=True)
    totals = jnp.sum(jnp.where(visible, jnp.exp(scores - highest), 0.0), -1, keepdims=True)
    log_total = highest + jnp.log(totals)
    probs_full = jnp.where(visible, jnp.exp(scores - log_total), 0.0)
    probs_round = probs_full.astype(bf16)
    attention = (
        jnp.einsum("kgts,skd->tkgd", probs_round, values, preferred_element_type=f32)
        .reshape(rows, hq)
        .astype(bf16)
    )

    if lows % 2 == 0:
        half = lax.dynamic_slice_in_dim(out_quarter, (ring.lo % 2) * (width // 2), width // 2, 0)
        near = jnp.stack(ring.gather(half)[1:])
        far = low_peer(near, 1)
        odd = (ring.lo % 2) != 0
        top = jnp.where(odd, far, near)
        bottom = jnp.where(odd, near, far)
        others = jnp.concatenate([top, bottom], 1)
        out_full = [out_quarter] + [others[i] for i in range(n - 1)]
    else:
        out_full = ring.gather(out_quarter)
    attn_blocks = [attention[i * block : (i + 1) * block] for i in range(n)]
    attn_rows = jnp.concatenate(xor_order(ring.exchange(attn_blocks), k), 1)
    projected = [dot(attn_rows, w) for w in out_full]
    mine_f = mine.astype(f32)
    middle = mine_f + jnp.concatenate(xor_order(projected, k), 1)
    inv_second = inverse_rms(middle)
    pre_second = middle * inv_second
    normed_mine = (pre_second * gain_second).astype(bf16)
    normed_second = jnp.concatenate(ring.gather(normed_mine), 0)
    ff = seqs * sub
    gate_w, up_w = gate_up[:, :ff], gate_up[:, ff:]
    gate_act = dot(normed_second, gate_w)
    up_proj = dot(normed_second, up_w)
    sigmoid = jax.nn.sigmoid(gate_act)
    hidden = (gate_act * sigmoid * up_proj).astype(bf16)

    def reduce_plane(partial):
        part = partial.astype(bf16)
        got = ring.exchange([part[i * block : (i + 1) * block] for i in range(n)])
        total = got[0].astype(f32)
        for value in got[1:]:
            total = total + value.astype(f32)
        return total

    grad_hidden = dot_t(all_cot, down)
    grad_gate = (grad_hidden * up_proj * sigmoid * (1.0 + gate_act * (1.0 - sigmoid))).astype(bf16)
    grad_up = (grad_hidden * gate_act * sigmoid).astype(bf16)
    normed_part = dot_t(grad_gate, gate_w) + dot_t(grad_up, up_w)
    grad_normed_second = reduce_plane(normed_part)
    grad_middle = norm_backward(
        grad_normed_second, pre_second, inv_second, gain_second, mine_cot.astype(f32)
    )
    grad_mid_round = grad_middle.astype(bf16)
    mid_quarters = xor_order(
        [grad_mid_round[:, i * width_out : (i + 1) * width_out] for i in range(n)], k
    )
    grad_attention = sum(dot_t(g, w) for g, w in zip(mid_quarters, out_full)).astype(bf16)
    grad_quarters = xor_order([grad_attention[:, i * hq : (i + 1) * hq] for i in range(n)], k)
    grad_attn = jnp.concatenate(ring.exchange(grad_quarters), 0)

    output = ring.collect((middle + reduce_plane(dot(hidden, down))).astype(bf16))
    sum_down = scatter_seq(dot_first(hidden, all_cot).astype(bf16))
    grad_gu = jnp.concatenate([grad_gate, grad_up], 1)
    sum_gu = scatter_seq(dot_first(normed_second, grad_gu).astype(bf16))
    gain_second_part = jnp.sum(grad_normed_second * pre_second, 0)

    grad_heads = grad_attn.reshape(rows, kvs, group_size, HD)
    delta = jnp.transpose(
        jnp.sum(
            grad_heads.astype(f32) * attention.astype(f32).reshape(rows, kvs, group_size, HD), -1
        ),
        (1, 2, 0),
    )
    grad_probs = jnp.einsum("tkgd,skd->kgts", grad_heads, values, preferred_element_type=f32)
    grad_scores = (factor * probs_full * (grad_probs - delta[..., None])).astype(bf16)
    grad_q_rot = jnp.einsum("kgts,skd->tkgd", grad_scores, keys, preferred_element_type=f32)
    grad_k_rot = jnp.einsum("kgts,tkgd->skd", grad_scores, query_heads, preferred_element_type=f32)
    grad_v = jnp.einsum("kgts,tkgd->skd", probs_round, grad_heads, preferred_element_type=f32)
    both_grad = jnp.concatenate(
        [grad_k_rot.reshape(length, hk), grad_v.reshape(length, hk)], 1
    ).astype(bf16)
    both_sum = both_grad[:rows].astype(f32)
    for e in range(1, lows):
        both_sum = both_sum + low_peer(both_grad[e * rows : (e + 1) * rows], e).astype(f32)
    grad_queries = (
        unrotate(grad_q_rot.reshape(rows, heads, HD), cosine, sine_table)
        .reshape(rows, hq)
        .astype(bf16)
    )
    grad_keys = (
        unrotate(both_sum[:, :hk].reshape(rows, kvs, HD), cosine, sine_table)
        .reshape(rows, hk)
        .astype(bf16)
    )
    grad_values = both_sum[:, hk:].astype(bf16)
    grad_qkv = jnp.concatenate([grad_queries, grad_keys, grad_values], 1)
    first_part = dot_t(grad_qkv, full_qkv[:, : hq + 2 * hk])
    gain_first_part = jnp.sum(first_part * pre_all, 0)

    turned = [
        jnp.concatenate([attn_blocks[e ^ i] for e in range(n)], 0) for i in range(n)
    ]
    attn_full = jnp.concatenate(xor_order(ring.exchange(turned), k), 1)
    mid_cols = jnp.concatenate(ring.exchange(mid_quarters), 0)
    gain_grad = jnp.pad(
        jnp.stack([gain_first_part, gain_second_part], 1).astype(bf16), ((0, 0), (0, 126))
    )
    last = jnp.concatenate(
        [
            dot_first(normed_first, grad_qkv).astype(bf16),
            dot_first(attn_full, mid_cols).astype(bf16),
            gain_grad,
        ],
        1,
    )
    sum_last = scatter_seq(last)

    grad_normed_first = reduce_plane(first_part)
    inv_first = inverse_rms(mine_f)
    grad_tokens = norm_backward(
        grad_normed_first, mine_f * inv_first, inv_first, gain_first, grad_middle
    ).astype(bf16)
    grad_tokens = ring.collect(grad_tokens)

    down_parts = xor_order(ring.gather(sum_down), k)
    gu_parts = xor_order(ring.gather(sum_gu), k)
    last_parts = xor_order(ring.gather(sum_last), k)
    grad_down = jnp.concatenate(down_parts, 0).astype(f32)

    def joined(parts, low, high):
        return jnp.concatenate([p[:, low:high] for p in parts], 1).astype(f32)

    def unit_joined(parts, low, high):
        split = [p[:, low:high].reshape(shard, seqs, 1, sub) for p in parts]
        return jnp.concatenate(split, 2).reshape(shard, seqs * n * sub).astype(f32)

    tail = hq + 2 * hk + width_out
    gain_sums = sum(p[:, tail:].astype(f32) for p in last_parts)
    return (
        output[None],
        grad_tokens[None],
        joined(last_parts, 0, hq),
        joined(last_parts, hq, hq + hk),
        joined(last_parts, hq + hk, hq + 2 * hk),
        joined(last_parts, hq + 2 * hk, tail),
        gain_sums[:, 0],
        unit_joined(gu_parts, 0, ff),
        unit_joined(gu_parts, ff, 2 * ff),
        grad_down,
        gain_sums[:, 1],
    )


def solution(mesh):
    return jax.shard_map(
        on_device,
        mesh=mesh,
        in_specs=(
            P("replica", "seq", None),
            P("replica", None),
            P("seq", None),
            P("seq", None),
            P("seq", None),
            P("seq", None),
            P("seq"),
            P("seq", None),
            P("seq", None),
            P("seq", None),
            P("seq"),
            P("replica", "seq", None),
        ),
        out_specs=(
            P("replica", "seq", None),
            P("replica", "seq", None),
            P("seq", None),
            P("seq", None),
            P("seq", None),
            P("seq", None),
            P("seq"),
            P("seq", None),
            P("seq", None),
            P("seq", None),
            P("seq"),
        ),
        check_vma=False,
    )
```
